32 devices in a mesh: seg: 8 (over z, y), blk: 4 (over x, core).
Axes of the slice: x: 2, y: 2, z: 4, core: 2. Of those that a mesh axis runs over, the one named last changes fastest.
Arguments:
- strain_rate: bfloat16 [2048, 16384], P('blk', 'seg'), may hold values from -1000 to 1000
- fir_taps: float32 [64], replicated, may hold values from -0.75 to 0.75
Outputs:
- correlation: float32 [2048, 2048, 128], P('blk', 'seg')
The draws below stay inside these ranges and needn't reach their ends.
All inputs are finite; a program needn't handle non-finite values.
Results may differ from the reference program's by a relative error of at most 0.0023.
Values may be sent and summed in bfloat16 or wider, within the bound.
No kernel may reach another device: no remote copies, remote signals or barrier semaphores. Data moves between devices by JAX's collectives and lax.ppermute only.
A program may use at most 256 MiB of HBM per device.

```python
import math
import jax
import jax.numpy as jnp
from jax import lax

CH = 2048
NFFT = 1024
NBIN = 128
FLO = 8
LAGS = 128
TAPS = 64
RAMW = 32
SEGS = 16
TIME = 16384


def draw_strain_rate(key, part):
    subkeys = jax.random.split(key, 6)
    block_count = SEGS
    lag_reach = 2 * LAGS
    slowness = jax.random.randint(subkeys[0], (block_count,), -2 * LAGS, 2 * LAGS + 1)
    delays = jnp.arange(CH, dtype=jnp.int32)[:, None] * slowness[None, :] // CH
    source = jax.random.normal(subkeys[1], (block_count, NFFT + 2 * lag_reach + 1), jnp.float32)
    positions = jnp.arange(NFFT, dtype=jnp.int32)[None, None, :] + delays[:, :, None] + lag_reach
    wavefield = source[jnp.arange(block_count, dtype=jnp.int32)[None, :, None], positions]
    strength = jax.random.uniform(subkeys[2], (1, block_count, 1), jnp.float32, 0.5, 2.0)
    coupling = jnp.exp(jax.random.uniform(subkeys[3], (CH, 1), jnp.float32, 0.0, 2.302585))
    background = jax.random.normal(subkeys[4], (CH, block_count, NFFT), jnp.float32)
    envelope = jnp.exp(jax.random.uniform(subkeys[5], (CH, TIME // (2 * RAMW)), jnp.float32, -1.203973, 1.098612))
    combined = (strength * wavefield + background).reshape(CH, TIME)
    envelope_full = jnp.repeat(envelope, 2 * RAMW, axis=1)
    return jnp.clip(coupling * envelope_full * combined, -1000.0, 1000.0).astype(jnp.bfloat16)


def normal_values(key, shape, width, reach, held_as=jnp.bfloat16):
    return jnp.clip(width * jax.random.normal(key, shape, jnp.float32), -reach, reach).astype(held_as)


def setup_inputs(seed: int = 0) -> dict:
    streams_of = jax.random.split(jax.random.key(seed), 3)
    strain_rate = draw_strain_rate(jax.random.fold_in(streams_of[2], 71), 0)
    fir_taps = normal_values(streams_of[1], (TAPS,), TAPS ** -0.5, 0.75, jnp.float32)
    return {"strain_rate": strain_rate, "fir_taps": fir_taps}


epsilon = 1e-06

def normalize(extended):
    window_len = 2 * RAMW + 1
    magnitude = jnp.abs(extended)
    running = lax.reduce_window(magnitude, jnp.zeros((), extended.dtype), lax.add, (1, window_len), (1, 1), 'VALID')
    return extended[:, RAMW:extended.shape[1] - RAMW] / (running / window_len + epsilon)

def band_matrix(fir_taps):
    rows_len = NFFT + TAPS
    padded = jnp.concatenate([fir_taps, jnp.zeros((rows_len + 2 - TAPS,), fir_taps.dtype)])
    tiled = jnp.tile(padded, NFFT // 2)[:NFFT // 2 * rows_len]
    return tiled.reshape(NFFT // 2, rows_len).T

def filter_blocks(normed, fir_taps):
    channels = normed.shape[0]
    groups = (normed.shape[1] - TAPS) // NFFT
    leading = normed[:, :groups * NFFT].reshape(channels, groups, NFFT)
    trailing = jnp.concatenate([leading[:, 1:, :TAPS], normed[:, None, groups * NFFT:]], axis=1)
    framed = jnp.concatenate([leading, trailing], axis=2)
    return jnp.einsum('cgw,wu->cgu', framed, band_matrix(fir_taps), precision=lax.Precision.HIGHEST)

def lag_table():
    freq_index = jnp.arange(NBIN, dtype=jnp.int32)[:, None] + FLO
    lag_index = jnp.arange(LAGS, dtype=jnp.int32)[None, :]
    phase_arg = (freq_index * lag_index % NFFT).astype(jnp.float32) * (2 * math.pi / NFFT)
    return jnp.cos(phase_arg)

def reference(strain_rate, fir_taps):
    margin = RAMW + TAPS // 2
    extended = jnp.pad(strain_rate.astype(jnp.float32), ((0, 0), (margin, NFFT + margin)))
    halves = filter_blocks(normalize(extended), fir_taps)
    frames = jnp.concatenate([halves[:, :-1], halves[:, 1:]], axis=2)
    spectrum = jnp.fft.rfft(frames, axis=2)[:, :, FLO:FLO + NBIN] / math.sqrt(NFFT)
    stacked = jnp.stack([spectrum.real.astype(jnp.bfloat16), spectrum.imag.astype(jnp.bfloat16)], axis=0)
    stacked = lax.optimization_barrier(stacked).astype(jnp.float32)
    flat_spec = jnp.transpose(stacked, (3, 0, 2, 1)).reshape(NBIN, 2 * SEGS, CH)
    block_len = 128 if CH % 128 == 0 else CH
    group_count = CH // block_len
    grouped = jnp.transpose(flat_spec.reshape(NBIN, 2 * SEGS, group_count, block_len), (2, 0, 1, 3))
    lag_cos = lag_table()

    def one_group(rows_spec):
        cross_spec = jnp.einsum('fki,fkj->fij', rows_spec, flat_spec, precision=lax.Precision.HIGHEST) / SEGS
        return jnp.einsum('fij,fl->ijl', cross_spec, lag_cos, precision=lax.Precision.HIGHEST) / NBIN
    result = lax.map(one_group, grouped)
    return result.reshape(CH, CH, LAGS)
```

```python
import functools
import math

import jax
import jax.numpy as jnp
import numpy as np
from jax import lax
from jax.experimental import pallas as pl
from jax.experimental.pallas import tpu as pltpu
from jax.sharding import PartitionSpec as P

NFFT = 1024
NBIN = 128
FLO = 8
LAGS = 128
TAPS = 64
RAMW = 32
HALF = NFFT // 2
EPSILON = 1e-06
LANE = 128
SPEC = 2 * NBIN
REACH = 10 * LANE
LEAD = LANE - TAPS // 2
GROUP = 8
GROUPS = NBIN // GROUP

bf16 = jnp.bfloat16
f32 = jnp.float32


def split(x):
    high = x.astype(bf16)
    return high, (x - high.astype(f32)).astype(bf16)


def half_dft_table():
    sample = np.arange(HALF)[:, None]
    freq = np.arange(NBIN)[None, :] + FLO
    phase = (sample * freq % NFFT) * (2 * math.pi / NFFT)
    table = np.stack([np.cos(phase), -np.sin(phase)], axis=2).reshape(HALF, SPEC) / math.sqrt(NFFT)
    return np.pad(table, ((32, 32), (0, 0))).astype(np.float32)


def lag_table(segs_total):
    freq = np.arange(NBIN)[:, None] + FLO
    lag = np.arange(LAGS)[None, :]
    table = np.cos((freq * lag % NFFT) * (2 * math.pi / NFFT)) / (segs_total * NBIN)
    high = table.astype(np.float32).astype(bf16)
    low = (table - high.astype(np.float64)).astype(np.float32).astype(bf16)
    row = np.concatenate([high, low], axis=1)
    return np.concatenate([row, row], axis=0)


def window_table():
    gap = np.arange(4 * LANE)[:, None] - LANE - np.arange(2 * LANE)[None, :]
    return (np.abs(gap) <= RAMW).astype(np.float32).astype(bf16)


def response_kernel(taps_ref, table_ref, high_ref, low_ref):
    row = lax.broadcasted_iota(jnp.int32, (64, 64), 0)
    col = lax.broadcasted_iota(jnp.int32, (64, 64), 1)
    index = row + 64 - 2 * col
    band = jnp.zeros((64, 64), f32)
    for k in range(TAPS):
        band = jnp.where(index == k, taps_ref[k], band)
    high_ref[...] = jnp.zeros_like(high_ref)
    low_ref[...] = jnp.zeros_like(low_ref)
    for block in range(17):
        part = jnp.dot(
            band,
            table_ref[32 * block : 32 * block + 64, :],
            precision=lax.Precision.HIGHEST,
            preferred_element_type=f32,
        )
        high, low = split(part)
        start = LEAD + 64 * block
        high_ref[start : start + 64, :] = high
        low_ref[start : start + 64, :] = low


def response(fir_taps):
    return pl.pallas_call(
        response_kernel,
        in_specs=[
            pl.BlockSpec(memory_space=pltpu.SMEM),
            pl.BlockSpec(memory_space=pltpu.VMEM),
        ],
        out_specs=[pl.BlockSpec(memory_space=pltpu.VMEM)] * 2,
        out_shape=[jax.ShapeDtypeStruct((REACH, SPEC), bf16)] * 2,
        name="response",
        cost_estimate=pl.CostEstimate(flops=2 * 6 * 64 * 64 * 17 * 256, bytes_accessed=2 << 20, transcendentals=0),
    )(fir_taps, jnp.asarray(half_dft_table()))


def spectrum_kernel(own_time, last_ref, left_ref, own_ref, right_ref, window_ref, high_ref, low_ref,
                    even_ref, first_ref, second_ref, normed_ref):
    rows = own_ref.shape[0]
    tiles = own_time // LANE + 2
    zero = jnp.zeros((rows, LANE), bf16)
    extended = jnp.concatenate([zero, left_ref[...], own_ref[...], right_ref[...], zero], axis=1)
    window = window_ref[...]
    for pair in range(tiles // 2):
        start = 2 * LANE * pair
        total = jnp.dot(
            jnp.abs(extended[:, start : start + 4 * LANE]), window, preferred_element_type=f32
        )
        centre = extended[:, start + LANE : start + 3 * LANE].astype(f32)
        normed_ref[:, start : start + 2 * LANE] = centre / (total * (1.0 / (2 * RAMW + 1)) + EPSILON)

    def transform(start, length):
        high, low = split(normed_ref[:, start : start + length])
        kept = high_ref[:length, :]
        out = jnp.dot(high, kept, preferred_element_type=f32)
        out += jnp.dot(low, kept, preferred_element_type=f32)
        out += jnp.dot(high, low_ref[:length, :], preferred_element_type=f32)
        return out.T

    freq = lax.broadcasted_iota(jnp.int32, (SPEC, rows), 0) // 2
    sign = jnp.where(lax.rem(freq, 2) == 0, 1.0, -1.0)
    first = transform(0, REACH)
    second = transform(NFFT, REACH)
    tail = transform(own_time, 2 * LANE)
    first_ref[...] = first
    even_ref[...] = (first + sign * second).astype(bf16)
    second_ref[...] = second + jnp.where(last_ref[0] == 1, sign * tail, jnp.zeros_like(tail))


def spectrum(last, left, own, right, high, low):
    channels, own_time = own.shape
    rows = min(128, channels)
    line = lambda i: (i, 0)
    whole = lambda i: (0, 0)
    across = lambda i: (0, i)
    return pl.pallas_call(
        functools.partial(spectrum_kernel, own_time),
        grid=(channels // rows,),
        in_specs=[
            pl.BlockSpec(memory_space=pltpu.SMEM),
            pl.BlockSpec((rows, LANE), line),
            pl.BlockSpec((rows, own_time), line),
            pl.BlockSpec((rows, LANE), line),
            pl.BlockSpec((4 * LANE, 2 * LANE), whole),
            pl.BlockSpec((REACH, SPEC), whole),
            pl.BlockSpec((REACH, SPEC), whole),
        ],
        out_specs=[pl.BlockSpec((SPEC, rows), across)] * 3,
        out_shape=[
            jax.ShapeDtypeStruct((SPEC, channels), bf16),
            jax.ShapeDtypeStruct((SPEC, channels), f32),
            jax.ShapeDtypeStruct((SPEC, channels), f32),
        ],
        scratch_shapes=[pltpu.VMEM((rows, own_time + 2 * LANE), f32)],
        compiler_params=pltpu.CompilerParams(vmem_limit_bytes=32 << 20),
        name="spectrum",
        cost_estimate=pl.CostEstimate(
            flops=2 * channels * SPEC * REACH * 6, bytes_accessed=6 << 20, transcendentals=0
        ),
    )(last, left, own, right, jnp.asarray(window_table()), high, low)


def correlate_kernel(pieces, rows, pitch, batch, *refs):
    row_refs = refs[:pieces]
    col_ref = refs[pieces]
    table_ref, out_ref, lhs_ref, cross_ref = refs[pieces + 1 :]
    width = col_ref.shape[2]
    depth = 2 * GROUP * pieces
    sub = lax.rem(pl.program_id(0), LANE // rows)

    @pl.when(sub == 0)
    def _():
        for g in range(GROUPS):
            part = jnp.concatenate([r[16 * g : 16 * g + 16, :] for r in row_refs], axis=0)
            lhs_ref[:, g * depth : (g + 1) * depth] = part.T

    lane = lax.broadcasted_iota(jnp.int32, (rows, depth), 1)
    freq = lax.rem(lane, 2 * GROUP) // 2
    start = pl.multiple_of(sub * rows, rows)
    for g in range(GROUPS):
        cols = jnp.concatenate([col_ref[d, 16 * g : 16 * g + 16, :] for d in range(pieces)], axis=0)
        part = lhs_ref[pl.ds(start, rows), g * depth : (g + 1) * depth]
        lhs = jnp.concatenate(
            [jnp.where(freq == q, part, jnp.zeros_like(part)) for q in range(GROUP)], axis=0
        )
        cross = jnp.dot(lhs, cols, preferred_element_type=f32)
        for q in range(GROUP):
            for h in range(width // LANE):
                base = (g * GROUP + q) * pitch
                cross_ref[h, base : base + rows, :] = cross[
                    q * rows : (q + 1) * rows, h * LANE : (h + 1) * LANE
                ]
    table = table_ref[...]

    def lags(b, carry):
        highs, lows = [], []
        for ii in range(batch):
            for h in range(width // LANE):
                by_freq = cross_ref[h, pl.ds(b * batch + ii, NBIN, stride=pitch), :]
                high, low = split(by_freq.T)
                highs.append(high)
                lows.append(low)
        lhs = jnp.concatenate([jnp.concatenate(highs, axis=0), jnp.concatenate(lows, axis=0)], axis=1)
        both = jnp.dot(lhs, table, preferred_element_type=f32)
        out = both[:, :LAGS] + both[:, LAGS:]
        out_ref[pl.ds(b * batch, batch)] = out.reshape(batch, width, LAGS)
        return carry

    lax.fori_loop(0, rows // batch, lags, 0)


def correlate(row_pieces, cols, table):
    pieces = len(row_pieces)
    channels = row_pieces[0].shape[1]
    width = cols.shape[2]
    rows, batch = 64, 16
    pitch = rows + 8
    per = LANE // rows
    return pl.pallas_call(
        functools.partial(correlate_kernel, pieces, rows, pitch, batch),
        grid=(channels // rows,),
        in_specs=[pl.BlockSpec((SPEC, LANE), lambda s: (0, s // per))] * pieces
        + [
            pl.BlockSpec((pieces, SPEC, width), lambda s: (0, 0, 0)),
            pl.BlockSpec((2 * NBIN, 2 * LAGS), lambda s: (0, 0)),
        ],
        out_specs=pl.BlockSpec((rows, width, LAGS), lambda s: (s, 0, 0)),
        out_shape=jax.ShapeDtypeStruct((channels, width, LAGS), f32),
        scratch_shapes=[
            pltpu.VMEM((LANE, SPEC * pieces), bf16),
            pltpu.VMEM((width // LANE, NBIN * pitch, LANE), f32),
        ],
        compiler_params=pltpu.CompilerParams(vmem_limit_bytes=56 << 20),
        name="correlate",
        cost_estimate=pl.CostEstimate(
            flops=2 * channels * width * NBIN * (256 + 512),
            bytes_accessed=channels * width * LAGS * 4,
            transcendentals=0,
        ),
    )(*row_pieces, cols, table)


def ring_pairs(count):
    order = list(range(0, count, 2)) + list(range(count - 1, 0, -2))
    forward = [(order[i], order[(i + 1) % count]) for i in range(count)]
    return forward, [(b, a) for a, b in forward]


def shards(strain_rate, fir_taps):
    channels, own_time = strain_rate.shape
    segs, blks = lax.axis_size("seg"), lax.axis_size("blk")
    seg, blk = lax.axis_index("seg"), lax.axis_index("blk")
    left = lax.ppermute(strain_rate[:, own_time - LANE :], "seg", [(i, i + 1) for i in range(segs - 1)])
    right = lax.ppermute(strain_rate[:, :LANE], "seg", [(i + 1, i) for i in range(segs - 1)])
    high, low = response(fir_taps)
    last = (seg == segs - 1).astype(jnp.int32).reshape(1)
    even, first, second = spectrum(last, left, strain_rate, right, high, low)
    following = lax.ppermute(first, "seg", [(i + 1, i) for i in range(segs - 1)])
    freq = lax.broadcasted_iota(jnp.int32, (SPEC, 1), 0) // 2
    odd = (second + jnp.where(freq % 2 == 0, 1.0, -1.0) * following).astype(bf16)

    forward, backward = ring_pairs(segs)
    row_pieces = []
    for own, steps in ((even, (segs // 2, segs - 1 - segs // 2)), (odd, (segs - 1 - segs // 2, segs // 2))):
        row_pieces.append(own)
        for pairs, count in zip((forward, backward), steps):
            moved = own
            for _ in range(count):
                moved = lax.ppermute(moved, "seg", pairs)
                row_pieces.append(moved)

    width = channels * blks // segs
    offset = (seg * width) % channels
    cols = jnp.stack([lax.dynamic_slice_in_dim(p, offset, width, 1) for p in row_pieces])
    owner = [s * width // channels for s in range(segs)]
    held = blk == (seg * width) // channels
    below = blks
    relation = jnp.bitwise_xor(blk, (seg * width) // channels)
    while below > 1:
        below //= 2
        pairs = []
        for s in range(segs):
            for high_bits in range(0, blks, 2 * below):
                source = owner[s] ^ high_bits
                pairs.append((s * blks + source, s * blks + (source ^ below)))
        moved = lax.ppermute(cols, ("seg", "blk"), pairs)
        cols = jnp.where(held, cols, moved)
        held = relation % below == 0
    return correlate(row_pieces, cols, jnp.asarray(lag_table(2 * segs)))


def solution(mesh):
    return jax.shard_map(
        shards,
        mesh=mesh,
        in_specs=(P("blk", "seg"), P()),
        out_specs=P("blk", "seg", None),
        check_vma=False,
    )
```

```python
import functools
import math

import jax
import jax.numpy as jnp
import numpy as np
from jax import lax
from jax.experimental import pallas as pl
from jax.experimental.pallas import tpu as pltpu
from jax.sharding import PartitionSpec as P

NFFT = 1024
NBIN = 128
FLO = 8
LAGS = 128
TAPS = 64
RAMW = 32
HALF = NFFT // 2
EPSILON = 1e-06
LANE = 128
SPEC = 2 * NBIN
REACH = 10 * LANE
LEAD = LANE - TAPS // 2
GROUP = 8
GROUPS = NBIN // GROUP

bf16 = jnp.bfloat16
f32 = jnp.float32


def split(x):
    high = x.astype(bf16)
    return high, (x - high.astype(f32)).astype(bf16)


def half_dft_table():
    sample = np.arange(HALF)[:, None]
    freq = np.arange(NBIN)[None, :] + FLO
    phase = (sample * freq % NFFT) * (2 * math.pi / NFFT)
    table = np.stack([np.cos(phase), -np.sin(phase)], axis=2).reshape(HALF, SPEC) / math.sqrt(NFFT)
    return np.pad(table, ((32, 32), (0, 0))).astype(np.float32)


def lag_table(segs_total):
    freq = np.arange(NBIN)[:, None] + FLO
    lag = np.arange(LAGS)[None, :]
    table = np.cos((freq * lag % NFFT) * (2 * math.pi / NFFT)) / (segs_total * NBIN)
    high = table.astype(np.float32).astype(bf16)
    low = (table - high.astype(np.float64)).astype(np.float32).astype(bf16)
    row = np.concatenate([high, low], axis=1)
    return np.concatenate([row, row], axis=0)


def window_table():
    gap = np.arange(4 * LANE)[:, None] - LANE - np.arange(2 * LANE)[None, :]
    return (np.abs(gap) <= RAMW).astype(np.float32).astype(bf16)


def response_kernel(taps_ref, table_ref, high_ref, low_ref):
    row = lax.broadcasted_iota(jnp.int32, (64, 64), 0)
    col = lax.broadcasted_iota(jnp.int32, (64, 64), 1)
    index = row + 64 - 2 * col
    band = jnp.zeros((64, 64), f32)
    for k in range(TAPS):
        band = jnp.where(index == k, taps_ref[k], band)
    high_ref[...] = jnp.zeros_like(high_ref)
    low_ref[...] = jnp.zeros_like(low_ref)
    for block in range(17):
        part = jnp.dot(
            band,
            table_ref[32 * block : 32 * block + 64, :],
            precision=lax.Precision.HIGHEST,
            preferred_element_type=f32,
        )
        high, low = split(part)
        start = LEAD + 64 * block
        high_ref[start : start + 64, :] = high
        low_ref[start : start + 64, :] = low


def response(fir_taps):
    return pl.pallas_call(
        response_kernel,
        in_specs=[
            pl.BlockSpec(memory_space=pltpu.SMEM),
            pl.BlockSpec(memory_space=pltpu.VMEM),
        ],
        out_specs=[pl.BlockSpec(memory_space=pltpu.VMEM)] * 2,
        out_shape=[jax.ShapeDtypeStruct((REACH, SPEC), bf16)] * 2,
        name="response",
        cost_estimate=pl.CostEstimate(flops=2 * 6 * 64 * 64 * 17 * 256, bytes_accessed=2 << 20, transcendentals=0),
    )(fir_taps, jnp.asarray(half_dft_table()))


def spectrum_kernel(own_time, last_ref, left_ref, own_ref, right_ref, window_ref, high_ref, low_ref,
                    even_ref, first_ref, second_ref, normed_ref):
    rows = own_ref.shape[0]
    tiles = own_time // LANE + 2
    zero = jnp.zeros((rows, LANE), bf16)
    extended = jnp.concatenate([zero, left_ref[...], own_ref[...], right_ref[...], zero], axis=1)
    window = window_ref[...]
    for pair in range(tiles // 2):
        start = 2 * LANE * pair
        total = jnp.dot(
            jnp.abs(extended[:, start : start + 4 * LANE]), window, preferred_element_type=f32
        )
        centre = extended[:, start + LANE : start + 3 * LANE].astype(f32)
        normed_ref[:, start : start + 2 * LANE] = centre / (total * (1.0 / (2 * RAMW + 1)) + EPSILON)

    def transform(start, length):
        high, low = split(normed_ref[:, start : start + length])
        kept = high_ref[:length, :]
        out = jnp.dot(high, kept, preferred_element_type=f32)
        out += jnp.dot(low, kept, preferred_element_type=f32)
        out += jnp.dot(high, low_ref[:length, :], preferred_element_type=f32)
        return out.T

    freq = lax.broadcasted_iota(jnp.int32, (SPEC, rows), 0) // 2
    sign = jnp.where(lax.rem(freq, 2) == 0, 1.0, -1.0)
    first = transform(0, REACH)
    second = transform(NFFT, REACH)
    tail = transform(own_time, 2 * LANE)
    first_ref[...] = first
    even_ref[...] = (first + sign * second).astype(bf16)
    second_ref[...] = second + jnp.where(last_ref[0] == 1, sign * tail, jnp.zeros_like(tail))


def spectrum(last, left, own, right, high, low):
    channels, own_time = own.shape
    rows = min(128, channels)
    line = lambda i: (i, 0)
    whole = lambda i: (0, 0)
    across = lambda i: (0, i)
    return pl.pallas_call(
        functools.partial(spectrum_kernel, own_time),
        grid=(channels // rows,),
        in_specs=[
            pl.BlockSpec(memory_space=pltpu.SMEM),
            pl.BlockSpec((rows, LANE), line),
            pl.BlockSpec((rows, own_time), line),
            pl.BlockSpec((rows, LANE), line),
            pl.BlockSpec((4 * LANE, 2 * LANE), whole),
            pl.BlockSpec((REACH, SPEC), whole),
            pl.BlockSpec((REACH, SPEC), whole),
        ],
        out_specs=[pl.BlockSpec((SPEC, rows), across)] * 3,
        out_shape=[
            jax.ShapeDtypeStruct((SPEC, channels), bf16),
            jax.ShapeDtypeStruct((SPEC, channels), f32),
            jax.ShapeDtypeStruct((SPEC, channels), f32),
        ],
        scratch_shapes=[pltpu.VMEM((rows, own_time + 2 * LANE), f32)],
        compiler_params=pltpu.CompilerParams(vmem_limit_bytes=60 << 20),
        name="spectrum",
        cost_estimate=pl.CostEstimate(
            flops=2 * channels * SPEC * REACH * 6, bytes_accessed=6 << 20, transcendentals=0
        ),
    )(last, left, own, right, jnp.asarray(window_table()), high, low)


def correlate_kernel(pieces, batches, rows, pitch, batch, *refs):
    row_refs = refs[:pieces]
    col_refs = refs[pieces : pieces + batches]
    table_ref, out_ref, lhs_ref, cross_ref = refs[pieces + batches :]
    width = out_ref.shape[1]
    depth = 2 * GROUP * pieces
    sub = lax.rem(pl.program_id(0), LANE // rows)

    @pl.when(sub == 0)
    def _():
        for g in range(GROUPS):
            part = jnp.concatenate([r[16 * g : 16 * g + 16, :] for r in row_refs], axis=0)
            lhs_ref[:, g * depth : (g + 1) * depth] = part.T

    lane = lax.broadcasted_iota(jnp.int32, (rows, depth), 1)
    freq = lax.rem(lane, 2 * GROUP) // 2
    start = pl.multiple_of(sub * rows, rows)
    for g in range(GROUPS):
        cols = jnp.concatenate(
            [r[d, 16 * g : 16 * g + 16, :] for r in col_refs for d in range(r.shape[0])], axis=0
        )
        part = lhs_ref[pl.ds(start, rows), g * depth : (g + 1) * depth]
        lhs = jnp.concatenate(
            [jnp.where(freq == q, part, jnp.zeros_like(part)) for q in range(GROUP)], axis=0
        )
        cross = jnp.dot(lhs, cols, preferred_element_type=f32)
        for q in range(GROUP):
            for h in range(width // LANE):
                base = (g * GROUP + q) * pitch
                cross_ref[h, base : base + rows, :] = cross[
                    q * rows : (q + 1) * rows, h * LANE : (h + 1) * LANE
                ]
    table = table_ref[...]

    def lags(b, carry):
        highs, lows = [], []
        for ii in range(batch):
            for h in range(width // LANE):
                by_freq = cross_ref[h, pl.ds(b * batch + ii, NBIN, stride=pitch), :]
                high, low = split(by_freq.T)
                highs.append(high)
                lows.append(low)
        lhs = jnp.concatenate([jnp.concatenate(highs, axis=0), jnp.concatenate(lows, axis=0)], axis=1)
        both = jnp.dot(lhs, table, preferred_element_type=f32)
        out = both[:, :LAGS] + both[:, LAGS:]
        out_ref[pl.ds(b * batch, batch)] = out.reshape(batch, width, LAGS)
        return carry

    lax.fori_loop(0, rows // batch, lags, 0)


def correlate(row_pieces, col_batches, table):
    pieces = len(row_pieces)
    channels = row_pieces[0].shape[1]
    width = col_batches[0].shape[2]
    rows, batch = 64, 32
    pitch = rows + 8
    per = LANE // rows
    return pl.pallas_call(
        functools.partial(correlate_kernel, pieces, len(col_batches), rows, pitch, batch),
        grid=(channels // rows,),
        in_specs=[pl.BlockSpec((SPEC, LANE), lambda s: (0, s // per))] * pieces
        + [pl.BlockSpec(c.shape, lambda s: (0, 0, 0)) for c in col_batches]
        + [pl.BlockSpec((2 * NBIN, 2 * LAGS), lambda s: (0, 0))],
        out_specs=pl.BlockSpec((rows, width, LAGS), lambda s: (s, 0, 0)),
        out_shape=jax.ShapeDtypeStruct((channels, width, LAGS), f32),
        scratch_shapes=[
            pltpu.VMEM((LANE, SPEC * pieces), bf16),
            pltpu.VMEM((width // LANE, NBIN * pitch, LANE), f32),
        ],
        compiler_params=pltpu.CompilerParams(vmem_limit_bytes=56 << 20),
        name="correlate",
        cost_estimate=pl.CostEstimate(
            flops=2 * channels * width * NBIN * (256 + 512),
            bytes_accessed=channels * width * LAGS * 4,
            transcendentals=0,
        ),
    )(*row_pieces, *col_batches, table)


def ring_pairs(count):
    order = list(range(0, count, 2)) + list(range(count - 1, 0, -2))
    forward = [(order[i], order[(i + 1) % count]) for i in range(count)]
    return forward, [(b, a) for a, b in forward]


def partner(row_pieces, segs, blks, seg, blk):
    channels = row_pieces[0].shape[1]
    width = channels * blks // segs
    offset = (seg * width) % channels
    cols = jnp.stack([lax.dynamic_slice_in_dim(p, offset, width, 1) for p in row_pieces])
    relation = jnp.bitwise_xor(blk, (seg * width) // channels)
    bit = blks
    while bit > 1:
        held = relation % bit == 0
        bit //= 2
        pairs = []
        for s in range(segs):
            for other in range(0, blks, 2 * bit):
                source = (s * width // channels) ^ other
                pairs.append((s * blks + source, s * blks + (source ^ bit)))
        cols = jnp.where(held, cols, lax.ppermute(cols, ("seg", "blk"), pairs))
    return cols


def shards(strain_rate, fir_taps):
    channels, own_time = strain_rate.shape
    segs, blks = lax.axis_size("seg"), lax.axis_size("blk")
    seg, blk = lax.axis_index("seg"), lax.axis_index("blk")
    left = lax.ppermute(strain_rate[:, own_time - LANE :], "seg", [(i, i + 1) for i in range(segs - 1)])
    right = lax.ppermute(strain_rate[:, :LANE], "seg", [(i + 1, i) for i in range(segs - 1)])
    high, low = response(fir_taps)
    last = (seg == segs - 1).astype(jnp.int32).reshape(1)
    even, first, second = spectrum(last, left, strain_rate, right, high, low)
    following = lax.ppermute(first, "seg", [(i + 1, i) for i in range(segs - 1)])
    freq = lax.broadcasted_iota(jnp.int32, (SPEC, 1), 0) // 2
    odd = (second + jnp.where(freq % 2 == 0, 1.0, -1.0) * following).astype(bf16)

    forward, backward = ring_pairs(segs)
    longer, shorter = segs // 2, segs - 1 - segs // 2
    early, late = [], []
    for own, steps, held_back in ((even, (longer, shorter), (1, 0)), (odd, (shorter, longer), (1, 2))):
        early.append(own)
        for pairs, count, after in zip((forward, backward), steps, held_back):
            moved = own
            for step in range(count):
                moved = lax.ppermute(moved, "seg", pairs)
                (early if step < count - after else late).append(moved)
    col_batches = [partner(batch, segs, blks, seg, blk) for batch in (early, late)]
    return correlate(early + late, col_batches, jnp.asarray(lag_table(2 * segs)))


def solution(mesh):
    return jax.shard_map(
        shards,
        mesh=mesh,
        in_specs=(P("blk", "seg"), P()),
        out_specs=P("blk", "seg", None),
        check_vma=False,
    )
```

```python
import functools
import math

import jax
import jax.numpy as jnp
import numpy as np
from jax import lax
from jax.experimental import pallas as pl
from jax.experimental.pallas import tpu as pltpu
from jax.sharding import PartitionSpec as P

NFFT = 1024
NBIN = 128
FLO = 8
LAGS = 128
TAPS = 64
RAMW = 32
HALF = NFFT // 2
EPSILON = 1e-06
LANE = 128
SPEC = 2 * NBIN
REACH = 10 * LANE
LEAD = LANE - TAPS // 2
GROUP = 8
GROUPS = NBIN // GROUP

bf16 = jnp.bfloat16
f32 = jnp.float32


def split(x):
    high = x.astype(bf16)
    return high, (x - high.astype(f32)).astype(bf16)


def half_dft_table():
    sample = np.arange(HALF)[:, None]
    freq = np.arange(NBIN)[None, :] + FLO
    phase = (sample * freq % NFFT) * (2 * math.pi / NFFT)
    table = np.stack([np.cos(phase), -np.sin(phase)], axis=2).reshape(HALF, SPEC) / math.sqrt(NFFT)
    return np.pad(table, ((32, 32), (0, 0))).astype(np.float32)


def lag_table(segs_total):
    freq = np.arange(NBIN)[:, None] + FLO
    lag = np.arange(LAGS)[None, :]
    table = np.cos((freq * lag % NFFT) * (2 * math.pi / NFFT)) / (segs_total * NBIN)
    high = table.astype(np.float32).astype(bf16)
    low = (table - high.astype(np.float64)).astype(np.float32).astype(bf16)
    row = np.concatenate([high, low], axis=1)
    return np.concatenate([row, row], axis=0)


def window_table():
    gap = np.arange(4 * LANE)[:, None] - LANE - np.arange(2 * LANE)[None, :]
    return (np.abs(gap) <= RAMW).astype(np.float32).astype(bf16)


def response_kernel(taps_ref, table_ref, high_ref, low_ref):
    row = lax.broadcasted_iota(jnp.int32, (64, 64), 0)
    col = lax.broadcasted_iota(jnp.int32, (64, 64), 1)
    index = row + 64 - 2 * col
    band = jnp.zeros((64, 64), f32)
    for k in range(TAPS):
        band = jnp.where(index == k, taps_ref[k], band)
    high_ref[...] = jnp.zeros_like(high_ref)
    low_ref[...] = jnp.zeros_like(low_ref)
    for block in range(17):
        part = jnp.dot(
            band,
            table_ref[32 * block : 32 * block + 64, :],
            precision=lax.Precision.HIGHEST,
            preferred_element_type=f32,
        )
        high, low = split(part)
        start = LEAD + 64 * block
        high_ref[start : start + 64, :] = high
        low_ref[start : start + 64, :] = low


def response(fir_taps):
    return pl.pallas_call(
        response_kernel,
        in_specs=[
            pl.BlockSpec(memory_space=pltpu.SMEM),
            pl.BlockSpec(memory_space=pltpu.VMEM),
        ],
        out_specs=[pl.BlockSpec(memory_space=pltpu.VMEM)] * 2,
        out_shape=[jax.ShapeDtypeStruct((REACH, SPEC), bf16)] * 2,
        name="response",
        cost_estimate=pl.CostEstimate(flops=2 * 6 * 64 * 64 * 17 * 256, bytes_accessed=2 << 20, transcendentals=0),
    )(fir_taps, jnp.asarray(half_dft_table()))


def normalize(extended, window, normed_ref):
    for start in range(0, extended.shape[1] - 2 * LANE, 2 * LANE):
        total = jnp.dot(
            jnp.abs(extended[:, start : start + 4 * LANE]), window, preferred_element_type=f32
        )
        centre = extended[:, start + LANE : start + 3 * LANE].astype(f32)
        normed_ref[:, start : start + 2 * LANE] = centre / (total * (1.0 / (2 * RAMW + 1)) + EPSILON)


def transform(normed, kept, rest):
    high, low = split(normed)
    out = jnp.dot(high, kept, preferred_element_type=f32)
    out += jnp.dot(low, kept, preferred_element_type=f32)
    out += jnp.dot(high, rest, preferred_element_type=f32)
    return out.T


def signs(shape):
    freq = lax.broadcasted_iota(jnp.int32, shape, 0) // 2
    return jnp.where(lax.rem(freq, 2) == 0, 1.0, -1.0)


def inner_kernel(own_ref, window_ref, high_ref, low_ref, first_ref, second_ref, normed_ref):
    normalize(own_ref[...], window_ref[...], normed_ref)
    edge = 2 * LANE
    first_ref[...] = transform(normed_ref[:, :NFFT], high_ref[edge:, :], low_ref[edge:, :])
    second_ref[...] = transform(
        normed_ref[:, NFFT - edge : 2 * NFFT - edge], high_ref[:NFFT, :], low_ref[:NFFT, :]
    )


def spectra_inner(own, tables):
    channels, own_time = own.shape
    rows = min(LANE, channels)
    whole = lambda i: (0, 0)
    return pl.pallas_call(
        inner_kernel,
        grid=(channels // rows,),
        in_specs=[
            pl.BlockSpec((rows, own_time), lambda i: (i, 0)),
            pl.BlockSpec((4 * LANE, 2 * LANE), whole),
            pl.BlockSpec((REACH, SPEC), whole),
            pl.BlockSpec((REACH, SPEC), whole),
        ],
        out_specs=[pl.BlockSpec((SPEC, rows), lambda i: (0, i))] * 2,
        out_shape=[jax.ShapeDtypeStruct((SPEC, channels), f32)] * 2,
        scratch_shapes=[pltpu.VMEM((rows, own_time - 2 * LANE), f32)],
        compiler_params=pltpu.CompilerParams(vmem_limit_bytes=60 << 20),
        name="spectra_inner",
        cost_estimate=pl.CostEstimate(
            flops=2 * channels * SPEC * REACH * 6, bytes_accessed=6 << 20, transcendentals=0
        ),
    )(own, jnp.asarray(window_table()), *tables)


def edge_kernel(last_ref, left_ref, head_ref, end_ref, right_ref, first_in, second_in, window_ref,
                high0_ref, low0_ref, high1_ref, low1_ref, first_ref, even_ref, second_ref, normed_ref):
    zero = jnp.zeros(right_ref.shape, bf16)
    window = window_ref[...]
    head, low_head = high0_ref[...], low0_ref[...]
    normalize(jnp.concatenate([zero, left_ref[...], head_ref[...]], axis=1), window, normed_ref)
    first = first_in[...] + transform(normed_ref[...], head, low_head)
    first_ref[...] = first
    normalize(jnp.concatenate([end_ref[...], right_ref[...], zero], axis=1), window, normed_ref)
    second = second_in[...] + transform(normed_ref[...], high1_ref[...], low1_ref[...])
    sign = signs(second.shape)
    even_ref[...] = (first + sign * second).astype(bf16)
    tail = transform(normed_ref[...], head, low_head)
    second_ref[...] = second + jnp.where(last_ref[0] == 1, sign * tail, jnp.zeros_like(tail))


def spectra_edge(last, left, own, right, first, second, tables):
    channels, own_time = own.shape
    rows = min(2 * LANE, channels)
    edge = 2 * LANE
    across = lambda i: (0, i)
    line = lambda i: (i, 0)
    high, low = tables
    return pl.pallas_call(
        edge_kernel,
        grid=(channels // rows,),
        in_specs=[
            pl.BlockSpec(memory_space=pltpu.SMEM),
            pl.BlockSpec((rows, LANE), line),
            pl.BlockSpec((rows, edge), line),
            pl.BlockSpec((rows, edge), lambda i: (i, own_time // edge - 1)),
            pl.BlockSpec((rows, LANE), line),
            pl.BlockSpec((SPEC, rows), across),
            pl.BlockSpec((SPEC, rows), across),
            pl.BlockSpec((2 * edge, edge), lambda i: (0, 0)),
            pl.BlockSpec((edge, SPEC), lambda i: (0, 0)),
            pl.BlockSpec((edge, SPEC), lambda i: (0, 0)),
            pl.BlockSpec((edge, SPEC), lambda i: (REACH // edge - 1, 0)),
            pl.BlockSpec((edge, SPEC), lambda i: (REACH // edge - 1, 0)),
        ],
        out_specs=[pl.BlockSpec((SPEC, rows), across)] * 3,
        out_shape=[jax.ShapeDtypeStruct((SPEC, channels), dtype) for dtype in (f32, bf16, f32)],
        scratch_shapes=[pltpu.VMEM((rows, edge), f32)],
        compiler_params=pltpu.CompilerParams(vmem_limit_bytes=60 << 20),
        name="spectra_edge",
        cost_estimate=pl.CostEstimate(
            flops=2 * channels * SPEC * edge * 9, bytes_accessed=4 << 20, transcendentals=0
        ),
    )(last, left, own, own, right, first, second, jnp.asarray(window_table()), high, low, high, low)


def correlate_kernel(pieces, batches, rows, pitch, batch, *refs):
    row_refs = refs[:pieces]
    col_refs = refs[pieces : pieces + batches]
    table_ref, out_ref, lhs_ref, cross_ref = refs[pieces + batches :]
    width = out_ref.shape[1]
    depth = 2 * GROUP * pieces
    sub = lax.rem(pl.program_id(0), LANE // rows)

    @pl.when(sub == 0)
    def _():
        for g in range(GROUPS):
            part = jnp.concatenate([r[16 * g : 16 * g + 16, :] for r in row_refs], axis=0)
            lhs_ref[:, g * depth : (g + 1) * depth] = part.T

    lane = lax.broadcasted_iota(jnp.int32, (rows, depth), 1)
    freq = lax.rem(lane, 2 * GROUP) // 2
    start = pl.multiple_of(sub * rows, rows)
    for g in range(GROUPS):
        cols = jnp.concatenate(
            [r[d, 16 * g : 16 * g + 16, :] for r in col_refs for d in range(r.shape[0])], axis=0
        )
        part = lhs_ref[pl.ds(start, rows), g * depth : (g + 1) * depth]
        lhs = jnp.concatenate(
            [jnp.where(freq == q, part, jnp.zeros_like(part)) for q in range(GROUP)], axis=0
        )
        cross = jnp.dot(lhs, cols, preferred_element_type=f32)
        for q in range(GROUP):
            for h in range(width // LANE):
                base = (g * GROUP + q) * pitch
                cross_ref[h, base : base + rows, :] = cross[
                    q * rows : (q + 1) * rows, h * LANE : (h + 1) * LANE
                ]
    table = table_ref[...]

    def lags(b, carry):
        highs, lows = [], []
        for ii in range(batch):
            for h in range(width // LANE):
                by_freq = cross_ref[h, pl.ds(b * batch + ii, NBIN, stride=pitch), :]
                high, low = split(by_freq.T)
                highs.append(high)
                lows.append(low)
        lhs = jnp.concatenate([jnp.concatenate(highs, axis=0), jnp.concatenate(lows, axis=0)], axis=1)
        both = jnp.dot(lhs, table, preferred_element_type=f32)
        out = both[:, :LAGS] + both[:, LAGS:]
        out_ref[pl.ds(b * batch, batch)] = out.reshape(batch, width, LAGS)
        return carry

    lax.fori_loop(0, rows // batch, lags, 0, unroll=2)


def correlate(row_pieces, col_batches, table):
    pieces = len(row_pieces)
    channels = row_pieces[0].shape[1]
    width = col_batches[0].shape[2]
    rows, batch = 64, 32
    pitch = rows + 8
    per = LANE // rows
    return pl.pallas_call(
        functools.partial(correlate_kernel, pieces, len(col_batches), rows, pitch, batch),
        grid=(channels // rows,),
        in_specs=[pl.BlockSpec((SPEC, LANE), lambda s: (0, s // per))] * pieces
        + [pl.BlockSpec(c.shape, lambda s: (0, 0, 0)) for c in col_batches]
        + [pl.BlockSpec((2 * NBIN, 2 * LAGS), lambda s: (0, 0))],
        out_specs=pl.BlockSpec((rows, width, LAGS), lambda s: (s, 0, 0)),
        out_shape=jax.ShapeDtypeStruct((channels, width, LAGS), f32),
        scratch_shapes=[
            pltpu.VMEM((LANE, SPEC * pieces), bf16),
            pltpu.VMEM((width // LANE, NBIN * pitch, LANE), f32),
        ],
        compiler_params=pltpu.CompilerParams(vmem_limit_bytes=56 << 20),
        name="correlate",
        cost_estimate=pl.CostEstimate(
            flops=2 * channels * width * NBIN * (256 + 512),
            bytes_accessed=channels * width * LAGS * 4,
            transcendentals=0,
        ),
    )(*row_pieces, *col_batches, table)


def ring_order(count):
    return list(range(0, count, 2)) + list(range(count - 1, 0, -2))


def ring_pairs(count):
    order = ring_order(count)
    forward = [(order[i], order[(i + 1) % count]) for i in range(count)]
    return forward, [(b, a) for a, b in forward]


def partner_width(channels, segs, blks):
    return channels * blks // segs


def partner(row_pieces, segs, blks, seg, blk):
    channels = row_pieces[0].shape[1]
    width = partner_width(channels, segs, blks)
    offset = (seg * width) % channels
    cols = jnp.stack([lax.dynamic_slice_in_dim(p, offset, width, 1) for p in row_pieces])
    relation = jnp.bitwise_xor(blk, (seg * width) // channels)
    bit = blks
    while bit > 1:
        held = relation % bit == 0
        bit //= 2
        pairs = []
        for s in range(segs):
            for other in range(0, blks, 2 * bit):
                source = (s * width // channels) ^ other
                pairs.append((s * blks + source, s * blks + (source ^ bit)))
        cols = jnp.where(held, cols, lax.ppermute(cols, ("seg", "blk"), pairs))
    return cols


def shards(strain_rate, fir_taps):
    own_time = strain_rate.shape[1]
    segs, blks = lax.axis_size("seg"), lax.axis_size("blk")
    seg, blk = lax.axis_index("seg"), lax.axis_index("blk")
    upward = [(i, i + 1) for i in range(segs - 1)]
    downward = [(i + 1, i) for i in range(segs - 1)]
    tables = response(fir_taps)
    source, tables = lax.optimization_barrier((strain_rate, tables))
    left = lax.ppermute(source[:, own_time - LANE :], "seg", upward)
    right = lax.ppermute(source[:, :LANE], "seg", downward)
    first, second = spectra_inner(strain_rate, tables)
    last = (seg == segs - 1).astype(jnp.int32).reshape(1)
    first, even, second = spectra_edge(last, left, strain_rate, right, first, second, tables)
    following = lax.ppermute(first, "seg", downward)
    odd = (second + signs((SPEC, 1)) * following).astype(bf16)
    even_later, odd = lax.optimization_barrier((even, odd))

    forward, backward = ring_pairs(segs)
    longer, shorter = segs // 2, segs - 1 - segs // 2
    early, middle, late = [even, odd], [], []
    chains = ((even, backward, longer, 0), (even_later, forward, shorter, 1),
              (odd, backward, longer, 1), (odd, forward, shorter, 1))
    for moved, pairs, count, lag in chains:
        for step in range(1, count + 1):
            moved = lax.ppermute(moved, "seg", pairs)
            if step + lag <= segs // 4:
                early.append(moved)
            else:
                (middle if step + lag < segs // 2 else late).append(moved)
    col_batches = [partner(batch, segs, blks, seg, blk) for batch in (early, middle, late)]
    return correlate(early + middle + late, col_batches, jnp.asarray(lag_table(2 * segs)))


def solution(mesh):
    return jax.shard_map(
        shards,
        mesh=mesh,
        in_specs=(P("blk", "seg"), P()),
        out_specs=P("blk", "seg", None),
        check_vma=False,
    )
```

```python
import functools
import math

import jax
import jax.numpy as jnp
import numpy as np
from jax import lax
from jax.experimental import pallas as pl
from jax.experimental.pallas import tpu as pltpu
from jax.sharding import PartitionSpec as P

NFFT = 1024
NBIN = 128
FLO = 8
LAGS = 128
TAPS = 64
RAMW = 32
HALF = NFFT // 2
EPSILON = 1e-06
LANE = 128
SPEC = 2 * NBIN
REACH = 10 * LANE
LEAD = LANE - TAPS // 2
GROUP = 8
GROUPS = NBIN // GROUP

bf16 = jnp.bfloat16
f32 = jnp.float32


def split(x):
    high = x.astype(bf16)
    return high, (x - high.astype(f32)).astype(bf16)


def half_dft_table():
    sample = np.arange(HALF)[:, None]
    freq = np.arange(NBIN)[None, :] + FLO
    phase = (sample * freq % NFFT) * (2 * math.pi / NFFT)
    table = np.stack([np.cos(phase), -np.sin(phase)], axis=2).reshape(HALF, SPEC) / math.sqrt(NFFT)
    return np.pad(table, ((32, 32), (0, 0))).astype(np.float32)


def lag_table(segs_total):
    freq = np.arange(NBIN)[:, None] + FLO
    lag = np.arange(LAGS)[None, :]
    table = np.cos((freq * lag % NFFT) * (2 * math.pi / NFFT)) / (segs_total * NBIN)
    high = table.astype(np.float32).astype(bf16)
    low = (table - high.astype(np.float64)).astype(np.float32).astype(bf16)
    row = np.concatenate([high, low], axis=1)
    return np.concatenate([row, row], axis=0)


def window_table():
    gap = np.arange(4 * LANE)[:, None] - LANE - np.arange(2 * LANE)[None, :]
    return (np.abs(gap) <= RAMW).astype(np.float32).astype(bf16)


def response_kernel(taps_ref, table_ref, high_ref, low_ref):
    row = lax.broadcasted_iota(jnp.int32, (64, 64), 0)
    col = lax.broadcasted_iota(jnp.int32, (64, 64), 1)
    index = row + 64 - 2 * col
    band = jnp.zeros((64, 64), f32)
    for k in range(TAPS):
        band = jnp.where(index == k, taps_ref[k], band)
    high_ref[...] = jnp.zeros_like(high_ref)
    low_ref[...] = jnp.zeros_like(low_ref)
    for block in range(17):
        part = jnp.dot(
            band,
            table_ref[32 * block : 32 * block + 64, :],
            precision=lax.Precision.HIGHEST,
            preferred_element_type=f32,
        )
        high, low = split(part)
        start = LEAD + 64 * block
        high_ref[start : start + 64, :] = high
        low_ref[start : start + 64, :] = low


def response(fir_taps):
    return pl.pallas_call(
        response_kernel,
        in_specs=[
            pl.BlockSpec(memory_space=pltpu.SMEM),
            pl.BlockSpec(memory_space=pltpu.VMEM),
        ],
        out_specs=[pl.BlockSpec(memory_space=pltpu.VMEM)] * 2,
        out_shape=[jax.ShapeDtypeStruct((REACH, SPEC), bf16)] * 2,
        name="response",
        cost_estimate=pl.CostEstimate(flops=2 * 6 * 64 * 64 * 17 * 256, bytes_accessed=2 << 20, transcendentals=0),
    )(fir_taps, jnp.asarray(half_dft_table()))


def normalize(extended, window, normed_ref):
    for start in range(0, extended.shape[1] - 2 * LANE, 2 * LANE):
        total = jnp.dot(
            jnp.abs(extended[:, start : start + 4 * LANE]), window, preferred_element_type=f32
        )
        centre = extended[:, start + LANE : start + 3 * LANE].astype(f32)
        normed_ref[:, start : start + 2 * LANE] = centre / (total * (1.0 / (2 * RAMW + 1)) + EPSILON)


def transform(normed, kept, rest):
    high, low = split(normed)
    out = jnp.dot(high, kept, preferred_element_type=f32)
    out += jnp.dot(low, kept, preferred_element_type=f32)
    out += jnp.dot(high, rest, preferred_element_type=f32)
    return out.T


def signs(shape):
    freq = lax.broadcasted_iota(jnp.int32, shape, 0) // 2
    return jnp.where(lax.rem(freq, 2) == 0, 1.0, -1.0)


def inner_kernel(own_ref, window_ref, high_ref, low_ref, first_ref, second_ref, normed_ref):
    normalize(own_ref[...], window_ref[...], normed_ref)
    edge = 2 * LANE
    first_ref[...] = transform(normed_ref[:, :NFFT], high_ref[edge:, :], low_ref[edge:, :])
    second_ref[...] = transform(
        normed_ref[:, NFFT - edge : 2 * NFFT - edge], high_ref[:NFFT, :], low_ref[:NFFT, :]
    )


def spectra_inner(own, tables):
    channels, own_time = own.shape
    rows = min(2 * LANE, channels)
    whole = lambda i: (0, 0)
    return pl.pallas_call(
        inner_kernel,
        grid=(channels // rows,),
        in_specs=[
            pl.BlockSpec((rows, own_time), lambda i: (i, 0)),
            pl.BlockSpec((4 * LANE, 2 * LANE), whole),
            pl.BlockSpec((REACH, SPEC), whole),
            pl.BlockSpec((REACH, SPEC), whole),
        ],
        out_specs=[pl.BlockSpec((SPEC, rows), lambda i: (0, i))] * 2,
        out_shape=[jax.ShapeDtypeStruct((SPEC, channels), f32)] * 2,
        scratch_shapes=[pltpu.VMEM((rows, own_time - 2 * LANE), f32)],
        compiler_params=pltpu.CompilerParams(vmem_limit_bytes=60 << 20),
        name="spectra_inner",
        cost_estimate=pl.CostEstimate(
            flops=2 * channels * SPEC * REACH * 6, bytes_accessed=6 << 20, transcendentals=0
        ),
    )(own, jnp.asarray(window_table()), *tables)


def edge_kernel(last_ref, left_ref, head_ref, end_ref, right_ref, first_in, second_in, window_ref,
                high0_ref, low0_ref, high1_ref, low1_ref, first_ref, even_ref, second_ref, normed_ref):
    zero = jnp.zeros(right_ref.shape, bf16)
    window = window_ref[...]
    head, low_head = high0_ref[...], low0_ref[...]
    normalize(jnp.concatenate([zero, left_ref[...], head_ref[...]], axis=1), window, normed_ref)
    first = first_in[...] + transform(normed_ref[...], head, low_head)
    first_ref[...] = first
    normalize(jnp.concatenate([end_ref[...], right_ref[...], zero], axis=1), window, normed_ref)
    second = second_in[...] + transform(normed_ref[...], high1_ref[...], low1_ref[...])
    sign = signs(second.shape)
    even_ref[...] = (first + sign * second).astype(bf16)
    tail = transform(normed_ref[...], head, low_head)
    second_ref[...] = second + jnp.where(last_ref[0] == 1, sign * tail, jnp.zeros_like(tail))


def spectra_edge(last, left, own, right, first, second, tables):
    channels, own_time = own.shape
    rows = min(2 * LANE, channels)
    edge = 2 * LANE
    across = lambda i: (0, i)
    line = lambda i: (i, 0)
    high, low = tables
    return pl.pallas_call(
        edge_kernel,
        grid=(channels // rows,),
        in_specs=[
            pl.BlockSpec(memory_space=pltpu.SMEM),
            pl.BlockSpec((rows, LANE), line),
            pl.BlockSpec((rows, edge), line),
            pl.BlockSpec((rows, edge), lambda i: (i, own_time // edge - 1)),
            pl.BlockSpec((rows, LANE), line),
            pl.BlockSpec((SPEC, rows), across),
            pl.BlockSpec((SPEC, rows), across),
            pl.BlockSpec((2 * edge, edge), lambda i: (0, 0)),
            pl.BlockSpec((edge, SPEC), lambda i: (0, 0)),
            pl.BlockSpec((edge, SPEC), lambda i: (0, 0)),
            pl.BlockSpec((edge, SPEC), lambda i: (REACH // edge - 1, 0)),
            pl.BlockSpec((edge, SPEC), lambda i: (REACH // edge - 1, 0)),
        ],
        out_specs=[pl.BlockSpec((SPEC, rows), across)] * 3,
        out_shape=[jax.ShapeDtypeStruct((SPEC, channels), dtype) for dtype in (f32, bf16, f32)],
        scratch_shapes=[pltpu.VMEM((rows, edge), f32)],
        compiler_params=pltpu.CompilerParams(vmem_limit_bytes=60 << 20),
        name="spectra_edge",
        cost_estimate=pl.CostEstimate(
            flops=2 * channels * SPEC * edge * 9, bytes_accessed=4 << 20, transcendentals=0
        ),
    )(last, left, own, own, right, first, second, jnp.asarray(window_table()), high, low, high, low)


def correlate_kernel(pieces, batches, rows, pitch, batch, *refs):
    row_refs = refs[:pieces]
    col_refs = refs[pieces : pieces + batches]
    table_ref, out_ref, lhs_ref, cross_ref = refs[pieces + batches :]
    width = out_ref.shape[1]
    depth = 2 * GROUP * pieces
    sub = lax.rem(pl.program_id(0), LANE // rows)

    @pl.when(sub == 0)
    def _():
        for g in range(GROUPS):
            part = jnp.concatenate([r[16 * g : 16 * g + 16, :] for r in row_refs], axis=0)
            lhs_ref[:, g * depth : (g + 1) * depth] = part.T

    lane = lax.broadcasted_iota(jnp.int32, (rows, depth), 1)
    freq = lax.rem(lane, 2 * GROUP) // 2
    start = pl.multiple_of(sub * rows, rows)
    for g in range(GROUPS):
        cols = jnp.concatenate(
            [r[d, 16 * g : 16 * g + 16, :] for r in col_refs for d in range(r.shape[0])], axis=0
        )
        part = lhs_ref[pl.ds(start, rows), g * depth : (g + 1) * depth]
        lhs = jnp.concatenate(
            [jnp.where(freq == q, part, jnp.zeros_like(part)) for q in range(GROUP)], axis=0
        )
        cross = jnp.dot(lhs, cols, preferred_element_type=f32)
        for q in range(GROUP):
            for h in range(width // LANE):
                base = (g * GROUP + q) * pitch
                cross_ref[h, base : base + rows, :] = cross[
                    q * rows : (q + 1) * rows, h * LANE : (h + 1) * LANE
                ]
    table = table_ref[...]

    def lags(b, carry):
        highs, lows = [], []
        for ii in range(batch):
            for h in range(width // LANE):
                by_freq = cross_ref[h, pl.ds(b * batch + ii, NBIN, stride=pitch), :]
                high, low = split(by_freq.T)
                highs.append(high)
                lows.append(low)
        lhs = jnp.concatenate([jnp.concatenate(highs, axis=0), jnp.concatenate(lows, axis=0)], axis=1)
        both = jnp.dot(lhs, table, preferred_element_type=f32)
        out = both[:, :LAGS] + both[:, LAGS:]
        out_ref[pl.ds(b * batch, batch)] = out.reshape(batch, width, LAGS)
        return carry

    lax.fori_loop(0, rows // batch, lags, 0, unroll=2)


def correlate(row_pieces, col_batches, table):
    pieces = len(row_pieces)
    channels = row_pieces[0].shape[1]
    width = col_batches[0].shape[2]
    rows, batch = 64, 32
    pitch = rows + 8
    per = LANE // rows
    return pl.pallas_call(
        functools.partial(correlate_kernel, pieces, len(col_batches), rows, pitch, batch),
        grid=(channels // rows,),
        in_specs=[pl.BlockSpec((SPEC, LANE), lambda s: (0, s // per))] * pieces
        + [pl.BlockSpec(c.shape, lambda s: (0, 0, 0)) for c in col_batches]
        + [pl.BlockSpec((2 * NBIN, 2 * LAGS), lambda s: (0, 0))],
        out_specs=pl.BlockSpec((rows, width, LAGS), lambda s: (s, 0, 0)),
        out_shape=jax.ShapeDtypeStruct((channels, width, LAGS), f32),
        scratch_shapes=[
            pltpu.VMEM((LANE, SPEC * pieces), bf16),
            pltpu.VMEM((width // LANE, NBIN * pitch, LANE), f32),
        ],
        compiler_params=pltpu.CompilerParams(vmem_limit_bytes=56 << 20),
        name="correlate",
        cost_estimate=pl.CostEstimate(
            flops=2 * channels * width * NBIN * (256 + 512),
            bytes_accessed=channels * width * LAGS * 4,
            transcendentals=0,
        ),
    )(*row_pieces, *col_batches, table)


def ring_order(count):
    return list(range(0, count, 2)) + list(range(count - 1, 0, -2))


def ring_pairs(count):
    order = ring_order(count)
    forward = [(order[i], order[(i + 1) % count]) for i in range(count)]
    return forward, [(b, a) for a, b in forward]


def partner_width(channels, segs, blks):
    return channels * blks // segs


def partner(row_pieces, segs, blks, seg, blk):
    channels = row_pieces[0].shape[1]
    width = partner_width(channels, segs, blks)
    offset = (seg * width) % channels
    cols = jnp.stack([lax.dynamic_slice_in_dim(p, offset, width, 1) for p in row_pieces])
    relation = jnp.bitwise_xor(blk, (seg * width) // channels)
    bit = blks
    while bit > 1:
        held = relation % bit == 0
        bit //= 2
        pairs = []
        for s in range(segs):
            for other in range(0, blks, 2 * bit):
                source = (s * width // channels) ^ other
                pairs.append((s * blks + source, s * blks + (source ^ bit)))
        cols = jnp.where(held, cols, lax.ppermute(cols, ("seg", "blk"), pairs))
    return cols


def shards(strain_rate, fir_taps):
    own_time = strain_rate.shape[1]
    segs, blks = lax.axis_size("seg"), lax.axis_size("blk")
    seg, blk = lax.axis_index("seg"), lax.axis_index("blk")
    upward = [(i, i + 1) for i in range(segs - 1)]
    downward = [(i + 1, i) for i in range(segs - 1)]
    tables = response(fir_taps)
    source, tables = lax.optimization_barrier((strain_rate, tables))
    left = lax.ppermute(source[:, own_time - LANE :], "seg", upward)
    right = lax.ppermute(source[:, :LANE], "seg", downward)
    first, second = spectra_inner(strain_rate, tables)
    last = (seg == segs - 1).astype(jnp.int32).reshape(1)
    first, even, second = spectra_edge(last, left, strain_rate, right, first, second, tables)
    following = lax.ppermute(first, "seg", downward)
    odd = (second + signs((SPEC, 1)) * following).astype(bf16)
    even_later, odd = lax.optimization_barrier((even, odd))

    forward, backward = ring_pairs(segs)
    longer, shorter = segs // 2, segs - 1 - segs // 2
    early, middle, late = [even, odd], [], []
    chains = ((even, backward, longer, 0), (even_later, forward, shorter, 1),
              (odd, backward, shorter, 1), (odd, forward, longer, 1))
    for moved, pairs, count, lag in chains:
        for step in range(1, count + 1):
            moved = lax.ppermute(moved, "seg", pairs)
            if lag == 0 and step == 1:
                moved = lax.optimization_barrier((moved, odd))[0]
            if step + lag <= segs // 4:
                early.append(moved)
            else:
                (middle if step + lag < segs // 2 else late).append(moved)
    col_batches = [partner(batch, segs, blks, seg, blk) for batch in (early, middle, late)]
    return correlate(early + middle + late, col_batches, jnp.asarray(lag_table(2 * segs)))


def solution(mesh):
    return jax.shard_map(
        shards,
        mesh=mesh,
        in_specs=(P("blk", "seg"), P()),
        out_specs=P("blk", "seg", None),
        check_vma=False,
    )
```

```python
import functools
import math

import jax
import jax.numpy as jnp
import numpy as np
from jax import lax
from jax.experimental import pallas as pl
from jax.experimental.pallas import tpu as pltpu
from jax.sharding import PartitionSpec as P

NFFT = 1024
NBIN = 128
FLO = 8
LAGS = 128
TAPS = 64
RAMW = 32
HALF = NFFT // 2
EPSILON = 1e-06
LANE = 128
SPEC = 2 * NBIN
REACH = 10 * LANE
LEAD = LANE - TAPS // 2
GROUP = 8
GROUPS = NBIN // GROUP

bf16 = jnp.bfloat16
f32 = jnp.float32


def split(x):
    high = x.astype(bf16)
    return high, (x - high.astype(f32)).astype(bf16)


def half_dft_table():
    sample = np.arange(HALF)[:, None]
    freq = np.arange(NBIN)[None, :] + FLO
    phase = (sample * freq % NFFT) * (2 * math.pi / NFFT)
    table = np.stack([np.cos(phase), -np.sin(phase)], axis=2).reshape(HALF, SPEC) / math.sqrt(NFFT)
    return np.pad(table, ((32, 32), (0, 0))).astype(np.float32)


def lag_table(segs_total):
    freq = np.arange(NBIN)[:, None] + FLO
    lag = np.arange(LAGS)[None, :]
    table = np.cos((freq * lag % NFFT) * (2 * math.pi / NFFT)) / (segs_total * NBIN)
    high = table.astype(np.float32).astype(bf16)
    low = (table - high.astype(np.float64)).astype(np.float32).astype(bf16)
    row = np.concatenate([high, low], axis=1)
    return np.concatenate([row, row], axis=0)


def window_table():
    gap = np.arange(4 * LANE)[:, None] - LANE - np.arange(2 * LANE)[None, :]
    return (np.abs(gap) <= RAMW).astype(np.float32).astype(bf16)


def response_kernel(taps_ref, table_ref, high_ref, low_ref):
    row = lax.broadcasted_iota(jnp.int32, (64, 64), 0)
    col = lax.broadcasted_iota(jnp.int32, (64, 64), 1)
    index = row + 64 - 2 * col
    band = jnp.zeros((64, 64), f32)
    for k in range(TAPS):
        band = jnp.where(index == k, taps_ref[k], band)
    high_ref[...] = jnp.zeros_like(high_ref)
    low_ref[...] = jnp.zeros_like(low_ref)
    for block in range(17):
        part = jnp.dot(
            band,
            table_ref[32 * block : 32 * block + 64, :],
            precision=lax.Precision.HIGHEST,
            preferred_element_type=f32,
        )
        high, low = split(part)
        start = LEAD + 64 * block
        high_ref[start : start + 64, :] = high
        low_ref[start : start + 64, :] = low


def response(fir_taps):
    return pl.pallas_call(
        response_kernel,
        in_specs=[
            pl.BlockSpec(memory_space=pltpu.SMEM),
            pl.BlockSpec(memory_space=pltpu.VMEM),
        ],
        out_specs=[pl.BlockSpec(memory_space=pltpu.VMEM)] * 2,
        out_shape=[jax.ShapeDtypeStruct((REACH, SPEC), bf16)] * 2,
        name="response",
        cost_estimate=pl.CostEstimate(flops=2 * 6 * 64 * 64 * 17 * 256, bytes_accessed=2 << 20, transcendentals=0),
    )(fir_taps, jnp.asarray(half_dft_table()))


def normalize(extended, window, normed_ref):
    for start in range(0, extended.shape[1] - 2 * LANE, 2 * LANE):
        total = jnp.dot(
            jnp.abs(extended[:, start : start + 4 * LANE]), window, preferred_element_type=f32
        )
        centre = extended[:, start + LANE : start + 3 * LANE].astype(f32)
        normed_ref[:, start : start + 2 * LANE] = centre / (total * (1.0 / (2 * RAMW + 1)) + EPSILON)


def transform(normed, kept, rest):
    high, low = split(normed)
    out = jnp.dot(high, kept, preferred_element_type=f32)
    out += jnp.dot(low, kept, preferred_element_type=f32)
    out += jnp.dot(high, rest, preferred_element_type=f32)
    return out.T


def signs(shape):
    freq = lax.broadcasted_iota(jnp.int32, shape, 0) // 2
    return jnp.where(lax.rem(freq, 2) == 0, 1.0, -1.0)


def inner_kernel(own_ref, window_ref, high_ref, low_ref, first_ref, second_ref, normed_ref):
    normalize(own_ref[...], window_ref[...], normed_ref)
    edge = 2 * LANE
    first_ref[...] = transform(normed_ref[:, :NFFT], high_ref[edge:, :], low_ref[edge:, :])
    second_ref[...] = transform(
        normed_ref[:, NFFT - edge : 2 * NFFT - edge], high_ref[:NFFT, :], low_ref[:NFFT, :]
    )


def spectra_inner(own, tables):
    channels, own_time = own.shape
    rows = min(2 * LANE, channels)
    whole = lambda i: (0, 0)
    return pl.pallas_call(
        inner_kernel,
        grid=(channels // rows,),
        in_specs=[
            pl.BlockSpec((rows, own_time), lambda i: (i, 0)),
            pl.BlockSpec((4 * LANE, 2 * LANE), whole),
            pl.BlockSpec((REACH, SPEC), whole),
            pl.BlockSpec((REACH, SPEC), whole),
        ],
        out_specs=[pl.BlockSpec((SPEC, rows), lambda i: (0, i))] * 2,
        out_shape=[jax.ShapeDtypeStruct((SPEC, channels), f32)] * 2,
        scratch_shapes=[pltpu.VMEM((rows, own_time - 2 * LANE), f32)],
        compiler_params=pltpu.CompilerParams(vmem_limit_bytes=60 << 20),
        name="spectra_inner",
        cost_estimate=pl.CostEstimate(
            flops=2 * channels * SPEC * REACH * 6, bytes_accessed=6 << 20, transcendentals=0
        ),
    )(own, jnp.asarray(window_table()), *tables)


def edge_kernel(last_ref, left_ref, head_ref, end_ref, right_ref, first_in, second_in, window_ref,
                high0_ref, low0_ref, high1_ref, low1_ref, first_ref, even_ref, second_ref, normed_ref):
    zero = jnp.zeros(right_ref.shape, bf16)
    window = window_ref[...]
    head, low_head = high0_ref[...], low0_ref[...]
    normalize(jnp.concatenate([zero, left_ref[...], head_ref[...]], axis=1), window, normed_ref)
    first = first_in[...] + transform(normed_ref[...], head, low_head)
    first_ref[...] = first
    normalize(jnp.concatenate([end_ref[...], right_ref[...], zero], axis=1), window, normed_ref)
    second = second_in[...] + transform(normed_ref[...], high1_ref[...], low1_ref[...])
    sign = signs(second.shape)
    even_ref[...] = (first + sign * second).astype(bf16)
    tail = transform(normed_ref[...], head, low_head)
    second_ref[...] = second + jnp.where(last_ref[0] == 1, sign * tail, jnp.zeros_like(tail))


def spectra_edge(last, left, own, right, first, second, tables):
    channels, own_time = own.shape
    rows = min(4 * LANE, channels)
    edge = 2 * LANE
    across = lambda i: (0, i)
    line = lambda i: (i, 0)
    high, low = tables
    return pl.pallas_call(
        edge_kernel,
        grid=(channels // rows,),
        in_specs=[
            pl.BlockSpec(memory_space=pltpu.SMEM),
            pl.BlockSpec((rows, LANE), line),
            pl.BlockSpec((rows, edge), line),
            pl.BlockSpec((rows, edge), lambda i: (i, own_time // edge - 1)),
            pl.BlockSpec((rows, LANE), line),
            pl.BlockSpec((SPEC, rows), across),
            pl.BlockSpec((SPEC, rows), across),
            pl.BlockSpec((2 * edge, edge), lambda i: (0, 0)),
            pl.BlockSpec((edge, SPEC), lambda i: (0, 0)),
            pl.BlockSpec((edge, SPEC), lambda i: (0, 0)),
            pl.BlockSpec((edge, SPEC), lambda i: (REACH // edge - 1, 0)),
            pl.BlockSpec((edge, SPEC), lambda i: (REACH // edge - 1, 0)),
        ],
        out_specs=[pl.BlockSpec((SPEC, rows), across)] * 3,
        out_shape=[jax.ShapeDtypeStruct((SPEC, channels), dtype) for dtype in (f32, bf16, f32)],
        scratch_shapes=[pltpu.VMEM((rows, edge), f32)],
        compiler_params=pltpu.CompilerParams(vmem_limit_bytes=60 << 20),
        name="spectra_edge",
        cost_estimate=pl.CostEstimate(
            flops=2 * channels * SPEC * edge * 9, bytes_accessed=4 << 20, transcendentals=0
        ),
    )(last, left, own, own, right, first, second, jnp.asarray(window_table()), high, low, high, low)


def correlate_kernel(pieces, batches, rows, pitch, steps, *refs):
    row_refs = refs[:pieces]
    col_refs = refs[pieces : pieces + batches]
    table_ref, out_ref, lhs_ref, even_ref, odd_ref = refs[pieces + batches :]
    width = out_ref.shape[1]
    depth = 2 * GROUP * pieces
    step = pl.program_id(0)
    sub = lax.rem(step, LANE // rows)
    parity = lax.rem(step, 2)
    start = pl.multiple_of(sub * rows, rows)

    @pl.when((sub == 0) & (step < steps))
    def _():
        for g in range(GROUPS):
            part = jnp.concatenate([r[16 * g : 16 * g + 16, :] for r in row_refs], axis=0)
            lhs_ref[:, g * depth : (g + 1) * depth] = part.T

    def cross_spectra(g, cross_ref):
        lane = lax.broadcasted_iota(jnp.int32, (rows, depth), 1)
        freq = lax.rem(lane, 2 * GROUP) // 2
        cols = jnp.concatenate(
            [r[d, 16 * g : 16 * g + 16, :] for r in col_refs for d in range(r.shape[0])], axis=0
        )
        part = lhs_ref[pl.ds(start, rows), g * depth : (g + 1) * depth]
        lhs = jnp.concatenate(
            [jnp.where(freq == q, part, jnp.zeros_like(part)) for q in range(GROUP)], axis=0
        )
        cross = jnp.dot(lhs, cols, preferred_element_type=f32)
        for q in range(GROUP):
            for h in range(width // LANE):
                base = (g * GROUP + q) * pitch
                cross_ref[h, base : base + rows, :] = cross[
                    q * rows : (q + 1) * rows, h * LANE : (h + 1) * LANE
                ]

    def lags(begin, count, cross_ref):
        highs, lows = [], []
        for i in range(begin, begin + count):
            for h in range(width // LANE):
                high, low = split(cross_ref[h, pl.ds(i, NBIN, stride=pitch), :].T)
                highs.append(high)
                lows.append(low)
        lhs = jnp.concatenate([jnp.concatenate(highs, axis=0), jnp.concatenate(lows, axis=0)], axis=1)
        both = jnp.dot(lhs, table_ref[...], preferred_element_type=f32)
        out = both[:, :LAGS] + both[:, LAGS:]
        out_ref[begin : begin + count] = out.reshape(count, width, LAGS)

    def run(into, source):
        quarter = GROUPS // 4
        for part in range(4):
            if into is not None:
                for g in range(part * quarter, (part + 1) * quarter):
                    cross_spectra(g, into)
            if source is not None:
                lags(part * (rows // 4), rows // 4, source)

    inside = (step > 0) & (step < steps)
    pl.when(step == 0)(lambda: run(even_ref, None))
    pl.when(inside & (parity == 0))(lambda: run(even_ref, odd_ref))
    pl.when(inside & (parity == 1))(lambda: run(odd_ref, even_ref))
    pl.when(step == steps)(lambda: run(None, odd_ref if steps % 2 == 0 else even_ref))


def correlate(row_pieces, col_batches, table):
    pieces = len(row_pieces)
    channels = row_pieces[0].shape[1]
    width = col_batches[0].shape[2]
    rows = 64
    pitch = rows + 8
    per = LANE // rows
    steps = channels // rows
    return pl.pallas_call(
        functools.partial(correlate_kernel, pieces, len(col_batches), rows, pitch, steps),
        grid=(steps + 1,),
        in_specs=[pl.BlockSpec((SPEC, LANE), lambda s: (0, jnp.minimum(s, steps - 1) // per))] * pieces
        + [pl.BlockSpec(c.shape, lambda s: (0, 0, 0), pipeline_mode=pl.Buffered(1)) for c in col_batches]
        + [pl.BlockSpec((2 * NBIN, 2 * LAGS), lambda s: (0, 0))],
        out_specs=pl.BlockSpec((rows, width, LAGS), lambda s: (jnp.maximum(s - 1, 0), 0, 0)),
        out_shape=jax.ShapeDtypeStruct((channels, width, LAGS), f32),
        scratch_shapes=[pltpu.VMEM((LANE, SPEC * pieces), bf16)]
        + [pltpu.VMEM((width // LANE, NBIN * pitch, LANE), f32)] * 2,
        compiler_params=pltpu.CompilerParams(vmem_limit_bytes=56 << 20),
        name="correlate",
        cost_estimate=pl.CostEstimate(
            flops=2 * channels * width * NBIN * (256 + 512),
            bytes_accessed=channels * width * LAGS * 4,
            transcendentals=0,
        ),
    )(*row_pieces, *col_batches, table)


def ring_order(count):
    return list(range(0, count, 2)) + list(range(count - 1, 0, -2))


def ring_pairs(count):
    order = ring_order(count)
    forward = [(order[i], order[(i + 1) % count]) for i in range(count)]
    return forward, [(b, a) for a, b in forward]


def partner_width(channels, segs, blks):
    return channels * blks // segs


def partner(row_pieces, segs, blks, seg, blk):
    channels = row_pieces[0].shape[1]
    width = partner_width(channels, segs, blks)
    offset = (seg * width) % channels
    cols = jnp.stack([lax.dynamic_slice_in_dim(p, offset, width, 1) for p in row_pieces])
    relation = jnp.bitwise_xor(blk, (seg * width) // channels)
    bit = blks
    while bit > 1:
        held = relation % bit == 0
        bit //= 2
        pairs = []
        for s in range(segs):
            for other in range(0, blks, 2 * bit):
                source = (s * width // channels) ^ other
                pairs.append((s * blks + source, s * blks + (source ^ bit)))
        cols = jnp.where(held, cols, lax.ppermute(cols, ("seg", "blk"), pairs))
    return cols


def shards(strain_rate, fir_taps):
    own_time = strain_rate.shape[1]
    segs, blks = lax.axis_size("seg"), lax.axis_size("blk")
    seg, blk = lax.axis_index("seg"), lax.axis_index("blk")
    upward = [(i, i + 1) for i in range(segs - 1)]
    downward = [(i + 1, i) for i in range(segs - 1)]
    tables = response(fir_taps)
    source, tables = lax.optimization_barrier((strain_rate, tables))
    left = lax.ppermute(source[:, own_time - LANE :], "seg", upward)
    right = lax.ppermute(source[:, :LANE], "seg", downward)
    first, second = spectra_inner(strain_rate, tables)
    last = (seg == segs - 1).astype(jnp.int32).reshape(1)
    first, even, second = spectra_edge(last, left, strain_rate, right, first, second, tables)
    following = lax.ppermute(first, "seg", downward)
    odd = (second + signs((SPEC, 1)) * following).astype(bf16)
    even_later, odd = lax.optimization_barrier((even, odd))

    forward, backward = ring_pairs(segs)
    longer, shorter = segs // 2, segs - 1 - segs // 2
    early, middle, late = [even, odd], [], []
    chains = ((even, backward, longer, 0), (even_later, forward, shorter, 1),
              (odd, backward, shorter, 1), (odd, forward, longer, 1))
    for moved, pairs, count, lag in chains:
        for step in range(1, count + 1):
            moved = lax.ppermute(moved, "seg", pairs)
            if lag == 0 and step == 1:
                moved = lax.optimization_barrier((moved, odd))[0]
            if step + lag <= segs // 4:
                early.append(moved)
            else:
                (middle if step + lag < segs // 2 else late).append(moved)
    col_batches = [partner(batch, segs, blks, seg, blk) for batch in (early, middle, late)]
    return correlate(early + middle + late, col_batches, jnp.asarray(lag_table(2 * segs)))


def solution(mesh):
    return jax.shard_map(
        shards,
        mesh=mesh,
        in_specs=(P("blk", "seg"), P()),
        out_specs=P("blk", "seg", None),
        check_vma=False,
    )
```
